32 devices in a mesh: row: 2 (over core), pitch: 4 (over y, x), span: 4 (over z).
Axes of the slice: x: 2, y: 2, z: 4, core: 2. Of those that a mesh axis runs over, the one named last changes fastest.
Arguments:
- snapshots: bfloat16 [2, 20, 3, 32, 256, 256], P('row', None, None, 'pitch', 'span'), may hold values from -6 to 6
- snap_index: int32 [16], replicated, may hold values from 0 to 19, as said below
- flow_state: float32 [2, 5, 32, 256, 256], P('row', None, 'pitch', 'span'), may hold values from -6 to 6
- eddy_viscosity: float32 [2, 32, 256, 256], P('row', 'pitch', 'span'), may hold values from 0.04 to 0.4
- intersection: int32 [2, 32], P('row'), may hold values from 0 to 31, as said below
- counts: int32 [2, 32], P('row'), may hold values from 1 to 8, as said below
Outputs:
- received_stress: float32 [2, 6, 256, 256], P('row', None, 'span')
- new_state: float32 [2, 5, 32, 256, 256], P('row', None, 'pitch', 'span')
The draws below stay inside these ranges and needn't reach their ends.
Inputs may be any that keep to these rules, and one draw needn't show every extreme that they name: `snap_index`: 16 distinct slots, among them slot 0 and slot 19. `intersection`: for each row, a one-to-one map of blocks. Call blocks k * 8 to (k + 1) * 8 - 1 group k: the blocks of one group take their sources from at most 2 blocks of any one group of the other layout, and exactly 2 for some pairs of groups. `counts`: each row has a block with all 8 cells live.
All inputs are finite; a program needn't handle non-finite values.
Results may differ from the reference program's by a relative error of at most 0.0003.
Values sent between devices are 32-bit elements; how exact they have to be, the bound alone decides.
A program may use at most 128 MiB of HBM per device.

```python
import math
import jax
import jax.numpy as jnp
from jax import lax

ROWS = 2
SNAPS = 16
SLOTS = 20
BLOCK = 8
BLK_DEV = 8
CAPACITY = 2
AXIAL = 256
NPITCH = 32
NSPAN = 256
NBLK = 32


def draw_snap_index(key, part):
    middle = jax.random.permutation(key, SLOTS - 2)[:SNAPS - 2] + 1
    chosen = jnp.concatenate([jnp.array([0, SLOTS - 1], dtype=jnp.int32), middle.astype(jnp.int32)])
    shuffle = jax.random.permutation(jax.random.fold_in(key, 7), SNAPS)
    return chosen[shuffle].astype(jnp.int32)


def draw_intersection(key, part):
    span_count = NBLK // BLK_DEV
    layouts = []
    for row_num in range(ROWS):
        row_key = jax.random.fold_in(key, 11 + row_num)
        offsets_base = jax.random.permutation(jax.random.fold_in(row_key, 1), span_count)[:BLK_DEV // CAPACITY]
        offsets = jnp.repeat(offsets_base, CAPACITY)
        offsets = offsets[jax.random.permutation(jax.random.fold_in(row_key, 2), BLK_DEV)]
        local_order = jax.random.permutation(jax.random.fold_in(row_key, 3), BLK_DEV)
        devices = jnp.arange(span_count, dtype=jnp.int32)
        source_dev = (devices[:, None] - offsets[None, :].astype(jnp.int32)) % span_count
        layouts.append((source_dev * BLK_DEV + local_order[None, :].astype(jnp.int32)).reshape(NBLK).astype(jnp.int32))
    return jnp.stack(layouts)


def draw_counts(key, part):
    values = jax.random.randint(key, (ROWS, NBLK), 1, BLOCK + 1)
    full_spot = jax.random.randint(jax.random.fold_in(key, 5), (ROWS, 1), 0, NBLK)
    return jnp.where(jnp.arange(NBLK)[None, :] == full_spot, BLOCK, values).astype(jnp.int32)


def block_levels(rng, extent, cuts, low, top_value):
    level, own = 1.0, jax.random.fold_in(rng, 6)
    for axis_at, parts in cuts:
        draws = jnp.exp(jax.random.uniform(jax.random.fold_in(own, axis_at), (parts,), jnp.float32, low / len(cuts), top_value / len(cuts)))
        level = level * jnp.repeat(draws, extent[axis_at] // parts).reshape([-1 if axis == axis_at else 1 for axis in range(len(extent))])
    return level


def scatter_about(stream_key, shape, scale, reach, split=(), kind=jnp.bfloat16):
    drawn = scale * jax.random.normal(stream_key, shape, jnp.float32)
    if split:
        drawn = drawn * block_levels(stream_key, shape, split, -0.22, 0.18)
    return jnp.clip(drawn, -reach, reach).astype(kind)


def setup_inputs(seed: int = 0) -> dict:
    seeds = jax.random.split(jax.random.key(seed), 7)
    snapshots = scatter_about(seeds[0], (ROWS, SLOTS, 3, NPITCH, NSPAN, AXIAL), 1.0, 6.0, ((0, 2), (3, 4), (4, 4)))
    snap_index = draw_snap_index(jax.random.fold_in(seeds[6], 71), 0)
    flow_state = scatter_about(seeds[2], (ROWS, 5, NPITCH, NSPAN, AXIAL), 1.0, 6.0, ((0, 2), (2, 4), (3, 4)), jnp.float32)
    eddy_viscosity = jnp.clip(jnp.exp(math.log(0.4) - 2.3025851 * jax.random.uniform(seeds[3], (ROWS, NPITCH, NSPAN, AXIAL), jnp.float32) ** block_levels(seeds[3], (ROWS, NPITCH, NSPAN, AXIAL), ((0, 2), (1, 4), (2, 4)), -0.2, 0.2)), 0.04, 0.4)
    intersection = draw_intersection(jax.random.fold_in(seeds[6], 71), 0)
    counts = draw_counts(jax.random.fold_in(seeds[6], 71), 0)
    return {"snapshots": snapshots, "snap_index": snap_index, "flow_state": flow_state, "eddy_viscosity": eddy_viscosity, "intersection": intersection, "counts": counts}


stress_pairs = ((0, 0), (0, 1), (0, 2), (1, 1), (1, 2), (2, 2))
time_step = 0.1


def axial_diff(values):
    padded = jnp.concatenate([values[..., :1], values, values[..., -1:]], axis=-1)
    return (padded[..., 2:] - padded[..., :-2]) * 0.5


def residual(flow_field, speed, viscosity, live_mask, forcing):
    pitch_pad = jnp.concatenate([flow_field[:, -1:], flow_field, flow_field[:, :1]], axis=1)
    span_pad = jnp.pad(flow_field, ((0, 0), (0, 0), (1, 1), (0, 0)))
    axial_pad = jnp.concatenate([flow_field[..., :1], flow_field, flow_field[..., -1:]], axis=3)
    laplace = (pitch_pad[:, 2:] + pitch_pad[:, :-2] + span_pad[:, :, 2:] + span_pad[:, :, :-2]
               + axial_pad[..., 2:] + axial_pad[..., :-2] - 6.0 * flow_field)
    return live_mask * (-axial_diff(speed * flow_field) + viscosity * laplace + forcing)


def row_stress(snaps_row, snap_index):
    def add_mean(running, slot):
        return running + snaps_row[slot].astype(jnp.float32), None

    zeros_three = jnp.zeros(snaps_row.shape[1:], jnp.float32)
    running, _ = lax.scan(add_mean, zeros_three, snap_index)
    time_mean = running / SNAPS

    def add_products(running, slot):
        fluct = snaps_row[slot].astype(jnp.float32) - time_mean
        products = jnp.stack([fluct[p] * fluct[q] for p, q in stress_pairs])
        return running + products, None

    zeros_six = jnp.zeros((6,) + snaps_row.shape[2:], jnp.float32)
    summed, _ = lax.scan(add_products, zeros_six, snap_index)
    cell_stress = summed / SNAPS
    return time_mean, jnp.sum(cell_stress, axis=1) / NPITCH


def reference(snapshots, snap_index, flow_state, eddy_viscosity, intersection, counts):
    means = []
    averaged = []
    for r in range(ROWS):
        time_mean, pitch_mean = row_stress(snapshots[r], snap_index)
        means.append(time_mean)
        averaged.append(pitch_mean)
    received = []
    for r in range(ROWS):
        source_row = averaged[1 - r].reshape(6, NBLK, BLOCK, AXIAL)
        received.append(jnp.take(source_row, intersection[r], axis=1).reshape(6, NSPAN, AXIAL))
    received_stress = jnp.stack(received)
    span_pos = (jnp.arange(NSPAN, dtype=jnp.float32) + 0.5) / NSPAN
    curvature = (1.0 / (1.0 + span_pos))[:, None]
    results = []
    for r in range(ROWS):
        stress_in = received[r]
        source_x = -axial_diff(stress_in[0]) - curvature * stress_in[1]
        source_r = -axial_diff(stress_in[1]) + curvature * (stress_in[5] - stress_in[3])
        source_t = -axial_diff(stress_in[2]) - 2.0 * curvature * stress_in[4]
        time_mean = means[r]
        energy = time_mean[0] * source_x + time_mean[1] * source_r + time_mean[2] * source_t
        forcing = jnp.concatenate([
            jnp.zeros((1, NPITCH, NSPAN, AXIAL), jnp.float32),
            jnp.broadcast_to(jnp.stack([source_x, source_r, source_t])[:, None], (3, NPITCH, NSPAN, AXIAL)),
            energy[None]], axis=0)
        live_mask = (jnp.arange(BLOCK, dtype=jnp.int32)[None, :] < counts[r][:, None]).astype(jnp.float32)
        live_mask = live_mask.reshape(NSPAN)[:, None]
        speed = 0.5 + time_mean[0]
        viscosity = eddy_viscosity[r]
        start = flow_state[r]
        section_one = start + time_step * residual(start, speed, viscosity, live_mask, forcing)
        results.append(0.5 * (start + section_one + time_step * residual(section_one, speed, viscosity, live_mask, forcing)))
    return received_stress, jnp.stack(results)
```

```python
import functools

import jax
import jax.numpy as jnp
from jax import lax
from jax.experimental import pallas as pl
from jax.experimental.pallas import tpu as pltpu
from jax.sharding import PartitionSpec as P

SNAPS = 16
BLOCK = 8
CAPACITY = 2
LANES = 128
ROWS_BF16 = 16
MESH = pl.DeviceIdType.MESH

stress_pairs = ((0, 0), (0, 1), (0, 2), (1, 1), (1, 2), (2, 2))
time_step = 0.1


def stress_kernel(*refs):
    snaps, (mean_ref, part_ref) = refs[1 : 1 + SNAPS], refs[1 + SNAPS :]
    cells = mean_ref.shape[1]
    halves = mean_ref.shape[3] // LANES
    for h in range(halves):
        cols = slice(h * LANES, (h + 1) * LANES)

        def one(i, acc):
            def load(t):
                return [snaps[t][0, 0, c, i, :, cols].astype(jnp.float32) for c in range(3)]

            base = load(0)
            sums, prods = None, None
            for t in range(1, SNAPS):
                now = load(t)
                d = [now[c] - base[c] for c in range(3)]
                pr = [d[p] * d[q] for p, q in stress_pairs]
                sums = d if sums is None else [a + b for a, b in zip(sums, d)]
                prods = pr if prods is None else [a + b for a, b in zip(prods, pr)]
            shift = [s * (1.0 / SNAPS) for s in sums]
            for c in range(3):
                mean_ref[c, i, :, cols] = base[c] + shift[c]
            return tuple(
                a + (pr - sums[p] * shift[q]) for a, pr, (p, q) in zip(acc, prods, stress_pairs)
            )

        zero = jnp.zeros((ROWS_BF16, LANES), jnp.float32)
        acc = lax.fori_loop(0, cells, one, (zero,) * 6)
        for m in range(6):
            part_ref[m * halves + h] = acc[m]
    for u in range(6 * halves, part_ref.shape[0]):
        part_ref[u] = jnp.zeros((ROWS_BF16, LANES), jnp.float32)


def stresses(snapshots, snap_index, units):
    _, _, comps, pitch, span, axial = snapshots.shape

    def spec(t):
        return pl.BlockSpec(
            (1, 1, comps, pitch, ROWS_BF16, axial), lambda j, idx: (0, idx[t], 0, 0, j, 0)
        )

    return pl.pallas_call(
        stress_kernel,
        out_shape=(
            jax.ShapeDtypeStruct((comps, pitch, span, axial), jnp.float32),
            jax.ShapeDtypeStruct((units, span, LANES), jnp.float32),
        ),
        grid_spec=pltpu.PrefetchScalarGridSpec(
            num_scalar_prefetch=1,
            grid=(span // ROWS_BF16,),
            in_specs=[spec(t) for t in range(SNAPS)],
            out_specs=(
                pl.BlockSpec((comps, pitch, ROWS_BF16, axial), lambda j, idx: (0, 0, j, 0)),
                pl.BlockSpec((units, ROWS_BF16, LANES), lambda j, idx: (0, j, 0)),
            ),
        ),
        cost_estimate=pl.CostEstimate(
            flops=SNAPS * 20 * pitch * span * axial,
            bytes_accessed=SNAPS * comps * pitch * span * axial * 2,
            transcendentals=0,
        ),
    )(snap_index, *([snapshots] * SNAPS))


def next_cell(x):
    lane = lax.broadcasted_iota(jnp.int32, x.shape, 1)
    return jnp.where(lane == x.shape[1] - 1, x, pltpu.roll(x, x.shape[1] - 1, 1))


def last_cell(x):
    lane = lax.broadcasted_iota(jnp.int32, x.shape, 1)
    return jnp.where(lane == 0, x, pltpu.roll(x, 1, 1))


def couple_kernel(
    n_p, n_s, scale,
    links, counts, part, low_face, q_hbm, mean_hbm, visc_hbm,
    rec_out, new_hbm,
    rs_buf, tot, out_buf, a2a, rec, qpad, spad, mean, visc, dtm, src,
    zsend, zrecv,
    rs_s, rs_r, aa_s, aa_r, ag_s, ag_r, hp_s, hp_r, hz_s, hz_r, loc, out_sem,
):
    r, p, s = lax.axis_index("row"), lax.axis_index("pitch"), lax.axis_index("span")
    comps, cells, span, axial = q_hbm.shape
    us = part.shape[0] // n_p
    blocks = span // BLOCK
    halves = axial // LANES
    tile = 16
    top = 8

    load_q = pltpu.make_async_copy(
        q_hbm, qpad.at[:, pl.ds(1, cells), pl.ds(top, span)], loc.at[0]
    )
    load_q.start()
    load_low = pltpu.make_async_copy(low_face, qpad.at[:, 0, pl.ds(top, span)], loc.at[1])
    load_low.start()
    load_mean = pltpu.make_async_copy(mean_hbm, mean, loc.at[2])
    load_mean.start()
    load_visc = pltpu.make_async_copy(visc_hbm, visc, loc.at[3])
    load_visc.start()

    barrier = pltpu.get_barrier_semaphore()
    for d in range(n_p):
        to = lax.rem(p + d, n_p)
        pl.semaphore_signal(barrier, inc=1, device_id=(1 - r, to, s), device_id_type=MESH)
        if d:
            pl.semaphore_signal(barrier, inc=1, device_id=(r, to, s), device_id_type=MESH)
    for d in range(1, n_s):
        to = lax.rem(s + d, n_s)
        pl.semaphore_signal(barrier, inc=1, device_id=(r, p, to), device_id_type=MESH)
    pl.semaphore_wait(barrier, 2 * n_p + n_s - 2)

    scatter = []
    for d in range(n_p):
        to = lax.rem(p + d, n_p)
        scatter.append(pltpu.make_async_remote_copy(
            src_ref=part.at[pl.ds(to * us, us)], dst_ref=rs_buf.at[d],
            send_sem=rs_s.at[d], recv_sem=rs_r.at[d],
            device_id=(1 - r, to, s), device_id_type=MESH,
        ))
    for copy in scatter:
        copy.start()
    right, left = lax.rem(p + 1, n_p), lax.rem(p + n_p - 1, n_p)
    above, below = lax.rem(s + 1, n_s), lax.rem(s + n_s - 1, n_s)
    high_q = pltpu.make_async_remote_copy(
        src_ref=q_hbm.at[:, 0], dst_ref=qpad.at[:, cells + 1, pl.ds(top, span)],
        send_sem=hp_s.at[0], recv_sem=hp_r.at[0],
        device_id=(r, left, s), device_id_type=MESH,
    )
    high_q.start()

    def span_faces(pad, k):
        def pack(i, carry):
            for c in range(comps):
                zsend[k, 0, c, pl.ds(i, 1)] = pad[c, i + 1, top + span - 1 : top + span]
                zsend[k, 1, c, pl.ds(i, 1)] = pad[c, i + 1, top : top + 1]
            return carry

        lax.fori_loop(0, cells, pack, 0)
        copies = []
        for way, to in ((0, above), (1, below)):
            copies.append(pltpu.make_async_remote_copy(
                src_ref=zsend.at[k, way], dst_ref=zrecv.at[k, way],
                send_sem=hz_s.at[k, way], recv_sem=hz_r.at[k, way],
                device_id=(r, p, to), device_id_type=MESH,
            ))
        for copy in copies:
            copy.start()
        return copies

    def span_land(pad, k):
        def land(i, carry):
            for c in range(comps):
                row = zrecv[k, 0, c, pl.ds(i, 1)]
                pad[c, i + 1, top - 1 : top] = jnp.where(s == 0, jnp.zeros_like(row), row)
                row = zrecv[k, 1, c, pl.ds(i, 1)]
                pad[c, i + 1, top + span : top + span + 1] = jnp.where(
                    s == n_s - 1, jnp.zeros_like(row), row
                )
            return carry

        lax.fori_loop(0, cells, land, 0)

    load_q.wait()
    load_low.wait()
    q_span = span_faces(qpad, 0)

    for j in range(span // tile):
        row = lax.broadcasted_iota(jnp.int32, (tile, axial), 0)
        first = counts[s * blocks + 2 * j]
        second = counts[s * blocks + 2 * j + 1]
        limit = jnp.where(row < BLOCK, first, second + BLOCK)
        dtm[j * tile : (j + 1) * tile] = jnp.where(row < limit, time_step, 0.0).astype(jnp.float32)

    for copy in scatter:
        copy.wait()
    for b in range(blocks):
        for u in range(us):
            total = rs_buf[0, u, b * BLOCK : (b + 1) * BLOCK]
            for d in range(1, n_p):
                total = total + rs_buf[d, u, b * BLOCK : (b + 1) * BLOCK]
            tot[u, b] = total * scale

    exchange = []
    for d in range(n_s):
        to = lax.rem(s + d, n_s)
        count = jnp.int32(0)
        picks = [jnp.int32(0)] * CAPACITY
        for k in range(blocks):
            block = links[to * blocks + k]
            here = block // blocks == s
            inside = block % blocks
            for c in range(CAPACITY):
                picks[c] = jnp.where(here & (count == c), inside, picks[c])
            count = count + here.astype(jnp.int32)
        for c in range(CAPACITY):
            for u in range(us):
                if d == 0:
                    a2a[0, c, u] = tot[u, picks[c]]
                else:
                    out_buf[d, c, u] = tot[u, picks[c]]
        if d:
            copy = pltpu.make_async_remote_copy(
                src_ref=out_buf.at[d], dst_ref=a2a.at[d],
                send_sem=aa_s.at[d], recv_sem=aa_r.at[d],
                device_id=(r, p, to), device_id_type=MESH,
            )
            copy.start()
            exchange.append(copy)
    sources = [links[s * blocks + k] // blocks for k in range(blocks)]
    for copy in exchange:
        copy.wait()
    for k in range(blocks):
        slot = jnp.int32(0)
        for e in range(k):
            slot = slot + (sources[e] == sources[k]).astype(jnp.int32)
        slot = jnp.minimum(slot, CAPACITY - 1)
        away = lax.rem(s - sources[k] + n_s, n_s)
        for u in range(us):
            rec[p * us + u, k * BLOCK : (k + 1) * BLOCK] = a2a[away, slot, u]
    gather = []
    for d in range(1, n_p):
        to = lax.rem(p + d, n_p)
        copy = pltpu.make_async_remote_copy(
            src_ref=rec.at[pl.ds(p * us, us)], dst_ref=rec.at[pl.ds(p * us, us)],
            send_sem=ag_s.at[d], recv_sem=ag_r.at[d],
            device_id=(r, to, s), device_id_type=MESH,
        )
        copy.start()
        gather.append(copy)

    for copy in q_span:
        copy.wait()
    span_land(qpad, 0)
    load_mean.wait()
    load_visc.wait()
    high_q.wait()
    for copy in gather:
        copy.wait()

    for j in range(span // tile):
        rows = slice(j * tile, (j + 1) * tile)
        t = [
            jnp.concatenate([rec[m * halves + h, rows] for h in range(halves)], axis=1)
            for m in range(6)
        ]
        for m in range(6):
            rec_out[m, rows] = t[m]
        row = lax.broadcasted_iota(jnp.int32, (tile, axial), 0) + (s * span + j * tile)
        curve = 1.0 / (1.0 + (row.astype(jnp.float32) + 0.5) / (span * n_s))
        diff = [(next_cell(t[m]) - last_cell(t[m])) * 0.5 for m in range(3)]
        live = dtm[rows]
        src[0, rows] = live * (-diff[0] - curve * t[1])
        src[1, rows] = live * (-diff[1] + curve * (t[5] - t[3]))
        src[2, rows] = live * (-diff[2] - 2.0 * curve * t[4])

    def section(pad, i, finish):
        for j in range(span // tile):
            rows = slice(j * tile, (j + 1) * tile)
            nu = visc[i, rows]
            means = [mean[c, i, rows] for c in range(3)]
            speed = 0.5 + means[0]
            live = dtm[rows]
            ahead = live * (nu - 0.5 * next_cell(speed))
            behind = live * (nu + 0.5 * last_cell(speed))
            nu = live * nu
            force = [src[c, rows] for c in range(3)]
            energy = means[0] * force[0] + means[1] * force[1] + means[2] * force[2]
            force = [None] + force + [energy]
            at = top + j * tile
            for c in range(comps):
                x = pad[c, i + 1, at : at + tile]
                around = (
                    pad[c, i, at : at + tile] + pad[c, i + 2, at : at + tile]
                    + pad[c, i + 1, at - 1 : at + tile - 1]
                    + pad[c, i + 1, at + 1 : at + tile + 1]
                )
                step = (
                    ahead * next_cell(x) + behind * last_cell(x) + nu * (around - 6.0 * x)
                )
                if force[c] is not None:
                    step = step + force[c]
                finish(c, i, at, x, step)

    def first(i, carry):
        def finish(c, i, at, x, step):
            spad[c, i + 1, at : at + tile] = x + step

        section(qpad, i, finish)
        return carry

    outs = []

    def second(i, carry):
        def finish(c, i, at, x, step):
            old = qpad[c, i + 1, at : at + tile]
            qpad[c, i + 1, at : at + tile] = 0.5 * (old + x + step)

        section(spad, i, finish)
        return carry

    inner = pl.ds(top, span)
    lax.fori_loop(0, 2, lambda e, carry: first(e * (cells - 1), carry), 0)
    faces = []
    for way, (mine, theirs, to) in enumerate(((cells, 0, right), (1, cells + 1, left))):
        copy = pltpu.make_async_remote_copy(
            src_ref=spad.at[:, mine, inner], dst_ref=spad.at[:, theirs, inner],
            send_sem=hp_s.at[1 + way], recv_sem=hp_r.at[1 + way],
            device_id=(r, to, s), device_id_type=MESH,
        )
        copy.start()
        faces.append(copy)
    lax.fori_loop(1, cells - 1, first, 0)
    s_span = span_faces(spad, 1)
    for copy in s_span:
        copy.wait()
    span_land(spad, 1)
    lax.fori_loop(1, cells - 1, second, 0)
    store_inner = pltpu.make_async_copy(
        qpad.at[:, pl.ds(2, cells - 2), inner], new_hbm.at[:, pl.ds(1, cells - 2)], out_sem.at[0]
    )
    store_inner.start()
    for copy in faces:
        copy.wait()
    lax.fori_loop(0, 2, lambda e, carry: second(e * (cells - 1), carry), 0)
    ends = []
    for e, i in enumerate((0, cells - 1)):
        copy = pltpu.make_async_copy(qpad.at[:, i + 1, inner], new_hbm.at[:, i], out_sem.at[1 + e])
        copy.start()
        ends.append(copy)
    store_inner.wait()
    for copy in ends:
        copy.wait()


def body(n_p, n_s, snapshots, snap_index, flow_state, eddy_viscosity, intersection, counts):
    start = flow_state[0]
    comps, cells, span, axial = start.shape
    halves = axial // LANES
    us = -(-6 * halves // n_p)
    units = us * n_p
    low_face = lax.ppermute(
        start[:, cells - 1], "pitch", [(i, (i + 1) % n_p) for i in range(n_p)]
    )
    mean, part = stresses(snapshots, snap_index, units)
    blocks = span // BLOCK
    f32 = jnp.float32
    pad = (comps, cells + 2, span + 16, axial)
    smem = pl.BlockSpec(memory_space=pltpu.SMEM)
    vmem = pl.BlockSpec(memory_space=pltpu.VMEM)
    hbm = pl.BlockSpec(memory_space=pl.ANY)
    dma = pltpu.SemaphoreType.DMA
    received, new = pl.pallas_call(
        functools.partial(couple_kernel, n_p, n_s, 1.0 / (SNAPS * cells * n_p)),
        out_shape=(
            jax.ShapeDtypeStruct((6, span, axial), f32),
            jax.ShapeDtypeStruct(start.shape, f32),
        ),
        in_specs=[smem, smem, vmem, hbm, hbm, hbm, hbm],
        out_specs=(vmem, hbm),
        scratch_shapes=[
            pltpu.VMEM((n_p, us, span, LANES), f32),
            pltpu.VMEM((us, blocks, BLOCK, LANES), f32),
            pltpu.VMEM((n_s, CAPACITY, us, BLOCK, LANES), f32),
            pltpu.VMEM((n_s, CAPACITY, us, BLOCK, LANES), f32),
            pltpu.VMEM((units, span, LANES), f32),
            pltpu.VMEM(pad, f32),
            pltpu.VMEM(pad, f32),
            pltpu.VMEM((3, cells, span, axial), f32),
            pltpu.VMEM((cells, span, axial), f32),
            pltpu.VMEM((span, axial), f32),
            pltpu.VMEM((3, span, axial), f32),
            pltpu.VMEM((2, 2, comps, cells, axial), f32),
            pltpu.VMEM((2, 2, comps, cells, axial), f32),
            dma((n_p,)), dma((n_p,)), dma((n_s,)), dma((n_s,)), dma((n_p,)), dma((n_p,)),
            dma((3,)), dma((3,)), dma((2, 2)), dma((2, 2)), dma((4,)), dma((3,)),
        ],
        compiler_params=pltpu.CompilerParams(
            collective_id=0, has_side_effects=True, vmem_limit_bytes=40 * 1024 * 1024
        ),
    )(intersection[0], counts[0], part, low_face, start, mean, eddy_viscosity[0])
    return (received[None], new[None])


def solution(mesh):
    return jax.shard_map(
        functools.partial(body, mesh.shape["pitch"], mesh.shape["span"]),
        mesh=mesh,
        in_specs=(
            P("row", None, None, "pitch", "span", None),
            P(),
            P("row", None, "pitch", "span", None),
            P("row", "pitch", "span", None),
            P("row", None),
            P("row", None),
        ),
        out_specs=(P("row", None, "span", None), P("row", None, "pitch", "span", None)),
        check_vma=False,
    )
```

```python
import functools

import jax
import jax.numpy as jnp
from jax import lax
from jax.experimental import pallas as pl
from jax.experimental.pallas import tpu as pltpu
from jax.sharding import PartitionSpec as P

SNAPS = 16
BLOCK = 8
CAPACITY = 2
LANES = 128
ROWS_BF16 = 16
MESH = pl.DeviceIdType.MESH

stress_pairs = ((0, 0), (0, 1), (0, 2), (1, 1), (1, 2), (2, 2))
time_step = 0.1


def stress_tile(snaps, slots, mean, part, rows):
    cells = mean.shape[1]
    halves = mean.shape[3] // LANES
    for h in range(halves):
        cols = slice(h * LANES, (h + 1) * LANES)

        def one(i, acc):
            def load(t):
                return [snaps[slots[t], c, i, :, cols].astype(jnp.float32) for c in range(3)]

            base = load(0)
            sums, prods = None, None
            for t in range(1, SNAPS):
                now = load(t)
                d = [now[c] - base[c] for c in range(3)]
                pr = [d[p] * d[q] for p, q in stress_pairs]
                sums = d if sums is None else [a + b for a, b in zip(sums, d)]
                prods = pr if prods is None else [a + b for a, b in zip(prods, pr)]
            shift = [s * (1.0 / SNAPS) for s in sums]
            for c in range(3):
                mean[c, i, rows, cols] = base[c] + shift[c]
            return tuple(
                a + (pr - sums[p] * shift[q]) for a, pr, (p, q) in zip(acc, prods, stress_pairs)
            )

        zero = jnp.zeros((ROWS_BF16, LANES), jnp.float32)
        acc = lax.fori_loop(0, cells, one, (zero,) * 6)
        for m in range(6):
            part[m * halves + h, rows] = acc[m]
    for u in range(6 * halves, part.shape[0]):
        part[u, rows] = jnp.zeros((ROWS_BF16, LANES), jnp.float32)


def next_cell(x):
    lane = lax.broadcasted_iota(jnp.int32, x.shape, 1)
    return jnp.where(lane == x.shape[1] - 1, x, pltpu.roll(x, x.shape[1] - 1, 1))


def last_cell(x):
    lane = lax.broadcasted_iota(jnp.int32, x.shape, 1)
    return jnp.where(lane == 0, x, pltpu.roll(x, 1, 1))


def couple_kernel(
    n_p, n_s, scale,
    slot_list, links, counts, snaps_hbm, q_hbm, visc_hbm,
    rec_out, new_hbm,
    snaps_even, snaps_odd, part, rs_buf, tot, out_buf, a2a, rec, qpad, spad, mean, visc, dtm, src,
    zsend, zrecv,
    rs_s, rs_r, aa_s, aa_r, ag_s, ag_r, hp_s, hp_r, hz_s, hz_r, loc, snap_sem, out_sem,
):
    r, p, s = lax.axis_index("row"), lax.axis_index("pitch"), lax.axis_index("span")
    comps, cells, span, axial = q_hbm.shape
    us = part.shape[0] // n_p
    blocks = span // BLOCK
    halves = axial // LANES
    tile = ROWS_BF16
    top = 8

    tiles = span // tile

    snaps = (snaps_even, snaps_odd)

    def load_snaps(j):
        return pltpu.make_async_copy(
            snaps_hbm.at[:, :, :, pl.ds(j * tile, tile)], snaps[j % 2], snap_sem.at[j]
        )

    loads = [load_snaps(j) for j in range(tiles)]
    loads[0].start()
    load_q = pltpu.make_async_copy(
        q_hbm, qpad.at[:, pl.ds(1, cells), pl.ds(top, span)], loc.at[0]
    )
    load_q.start()
    load_visc = pltpu.make_async_copy(visc_hbm, visc, loc.at[1])
    load_visc.start()
    loads[1].start()

    barrier = pltpu.get_barrier_semaphore()
    for d in range(n_p):
        to = lax.rem(p + d, n_p)
        pl.semaphore_signal(barrier, inc=1, device_id=(1 - r, to, s), device_id_type=MESH)
        if d:
            pl.semaphore_signal(barrier, inc=1, device_id=(r, to, s), device_id_type=MESH)
    for d in range(1, n_s):
        to = lax.rem(s + d, n_s)
        pl.semaphore_signal(barrier, inc=1, device_id=(r, p, to), device_id_type=MESH)
    pl.semaphore_wait(barrier, 2 * n_p + n_s - 2)

    right, left = lax.rem(p + 1, n_p), lax.rem(p + n_p - 1, n_p)
    above, below = lax.rem(s + 1, n_s), lax.rem(s + n_s - 1, n_s)
    high_q = pltpu.make_async_remote_copy(
        src_ref=q_hbm.at[:, 0], dst_ref=qpad.at[:, cells + 1, pl.ds(top, span)],
        send_sem=hp_s.at[0], recv_sem=hp_r.at[0],
        device_id=(r, left, s), device_id_type=MESH,
    )
    low_q = pltpu.make_async_remote_copy(
        src_ref=q_hbm.at[:, cells - 1], dst_ref=qpad.at[:, 0, pl.ds(top, span)],
        send_sem=hp_s.at[3], recv_sem=hp_r.at[3],
        device_id=(r, right, s), device_id_type=MESH,
    )
    low_q.start()

    def span_faces(pad, k):
        def pack(i, carry):
            for c in range(comps):
                zsend[k, 0, c, pl.ds(i, 1)] = pad[c, i + 1, top + span - 1 : top + span]
                zsend[k, 1, c, pl.ds(i, 1)] = pad[c, i + 1, top : top + 1]
            return carry

        lax.fori_loop(0, cells, pack, 0)
        copies = []
        for way, to in ((0, above), (1, below)):
            copies.append(pltpu.make_async_remote_copy(
                src_ref=zsend.at[k, way], dst_ref=zrecv.at[k, way],
                send_sem=hz_s.at[k, way], recv_sem=hz_r.at[k, way],
                device_id=(r, p, to), device_id_type=MESH,
            ))
        for copy in copies:
            copy.start()
        return copies

    def span_land(pad, k):
        def land(i, carry):
            for c in range(comps):
                row = zrecv[k, 0, c, pl.ds(i, 1)]
                pad[c, i + 1, top - 1 : top] = jnp.where(s == 0, jnp.zeros_like(row), row)
                row = zrecv[k, 1, c, pl.ds(i, 1)]
                pad[c, i + 1, top + span : top + span + 1] = jnp.where(
                    s == n_s - 1, jnp.zeros_like(row), row
                )
            return carry

        lax.fori_loop(0, cells, land, 0)

    load_q.wait()
    q_span = span_faces(qpad, 0)

    slots = [slot_list[t] for t in range(SNAPS)]
    scatter = []
    for j in range(tiles):
        loads[j].wait()
        stress_tile(snaps[j % 2], slots, mean, part, slice(j * tile, (j + 1) * tile))
        if j + 2 < tiles:
            loads[j + 2].start()
        for d in range(n_p):
            to = lax.rem(p + d, n_p)
            copy = pltpu.make_async_remote_copy(
                src_ref=part.at[pl.ds(to * us, us), pl.ds(j * tile, tile)],
                dst_ref=rs_buf.at[d, :, pl.ds(j * tile, tile)],
                send_sem=rs_s.at[d, j], recv_sem=rs_r.at[d, j],
                device_id=(1 - r, to, s), device_id_type=MESH,
            )
            copy.start()
            scatter.append(copy)
    high_q.start()

    for j in range(span // tile):
        row = lax.broadcasted_iota(jnp.int32, (tile, axial), 0)
        first = counts[s * blocks + 2 * j]
        second = counts[s * blocks + 2 * j + 1]
        limit = jnp.where(row < BLOCK, first, second + BLOCK)
        dtm[j * tile : (j + 1) * tile] = jnp.where(row < limit, time_step, 0.0).astype(jnp.float32)

    for copy in scatter:
        copy.wait()
    for b in range(blocks):
        for u in range(us):
            total = rs_buf[0, u, b * BLOCK : (b + 1) * BLOCK]
            for d in range(1, n_p):
                total = total + rs_buf[d, u, b * BLOCK : (b + 1) * BLOCK]
            tot[u, b] = total * scale

    exchange = []
    for d in range(n_s):
        to = lax.rem(s + d, n_s)
        count = jnp.int32(0)
        picks = [jnp.int32(0)] * CAPACITY
        for k in range(blocks):
            block = links[to * blocks + k]
            here = block // blocks == s
            inside = block % blocks
            for c in range(CAPACITY):
                picks[c] = jnp.where(here & (count == c), inside, picks[c])
            count = count + here.astype(jnp.int32)
        for c in range(CAPACITY):
            for u in range(us):
                if d == 0:
                    a2a[0, c, u] = tot[u, picks[c]]
                else:
                    out_buf[d, c, u] = tot[u, picks[c]]
        if d:
            copy = pltpu.make_async_remote_copy(
                src_ref=out_buf.at[d], dst_ref=a2a.at[d],
                send_sem=aa_s.at[d], recv_sem=aa_r.at[d],
                device_id=(r, p, to), device_id_type=MESH,
            )
            copy.start()
            exchange.append(copy)
    sources = [links[s * blocks + k] // blocks for k in range(blocks)]
    for copy in exchange:
        copy.wait()
    for k in range(blocks):
        slot = jnp.int32(0)
        for e in range(k):
            slot = slot + (sources[e] == sources[k]).astype(jnp.int32)
        slot = jnp.minimum(slot, CAPACITY - 1)
        away = lax.rem(s - sources[k] + n_s, n_s)
        for u in range(us):
            rec[p * us + u, k * BLOCK : (k + 1) * BLOCK] = a2a[away, slot, u]
    gather = []
    for d in range(1, n_p):
        to = lax.rem(p + d, n_p)
        copy = pltpu.make_async_remote_copy(
            src_ref=rec.at[pl.ds(p * us, us)], dst_ref=rec.at[pl.ds(p * us, us)],
            send_sem=ag_s.at[d], recv_sem=ag_r.at[d],
            device_id=(r, to, s), device_id_type=MESH,
        )
        copy.start()
        gather.append(copy)

    for copy in q_span:
        copy.wait()
    span_land(qpad, 0)
    load_visc.wait()
    low_q.wait()
    high_q.wait()
    for copy in gather:
        copy.wait()

    for j in range(span // tile):
        rows = slice(j * tile, (j + 1) * tile)
        t = [
            jnp.concatenate([rec[m * halves + h, rows] for h in range(halves)], axis=1)
            for m in range(6)
        ]
        for m in range(6):
            rec_out[m, rows] = t[m]
        row = lax.broadcasted_iota(jnp.int32, (tile, axial), 0) + (s * span + j * tile)
        curve = 1.0 / (1.0 + (row.astype(jnp.float32) + 0.5) / (span * n_s))
        diff = [(next_cell(t[m]) - last_cell(t[m])) * 0.5 for m in range(3)]
        live = dtm[rows]
        src[0, rows] = live * (-diff[0] - curve * t[1])
        src[1, rows] = live * (-diff[1] + curve * (t[5] - t[3]))
        src[2, rows] = live * (-diff[2] - 2.0 * curve * t[4])

    def section(pad, i, finish):
        for j in range(span // tile):
            rows = slice(j * tile, (j + 1) * tile)
            nu = visc[i, rows]
            means = [mean[c, i, rows] for c in range(3)]
            speed = 0.5 + means[0]
            live = dtm[rows]
            ahead = live * (nu - 0.5 * next_cell(speed))
            behind = live * (nu + 0.5 * last_cell(speed))
            nu = live * nu
            force = [src[c, rows] for c in range(3)]
            energy = means[0] * force[0] + means[1] * force[1] + means[2] * force[2]
            force = [None] + force + [energy]
            at = top + j * tile
            for c in range(comps):
                x = pad[c, i + 1, at : at + tile]
                around = (
                    pad[c, i, at : at + tile] + pad[c, i + 2, at : at + tile]
                    + pad[c, i + 1, at - 1 : at + tile - 1]
                    + pad[c, i + 1, at + 1 : at + tile + 1]
                )
                step = (
                    ahead * next_cell(x) + behind * last_cell(x) + nu * (around - 6.0 * x)
                )
                if force[c] is not None:
                    step = step + force[c]
                finish(c, i, at, x, step)

    def first(i, carry):
        def finish(c, i, at, x, step):
            spad[c, i + 1, at : at + tile] = x + step

        section(qpad, i, finish)
        return carry

    outs = []

    def second(i, carry):
        def finish(c, i, at, x, step):
            old = qpad[c, i + 1, at : at + tile]
            qpad[c, i + 1, at : at + tile] = 0.5 * (old + x + step)

        section(spad, i, finish)
        return carry

    inner = pl.ds(top, span)
    lax.fori_loop(0, 2, lambda e, carry: first(e * (cells - 1), carry), 0)
    faces = []
    for way, (mine, theirs, to) in enumerate(((cells, 0, right), (1, cells + 1, left))):
        copy = pltpu.make_async_remote_copy(
            src_ref=spad.at[:, mine, inner], dst_ref=spad.at[:, theirs, inner],
            send_sem=hp_s.at[1 + way], recv_sem=hp_r.at[1 + way],
            device_id=(r, to, s), device_id_type=MESH,
        )
        copy.start()
        faces.append(copy)
    lax.fori_loop(1, cells - 1, first, 0)
    s_span = span_faces(spad, 1)
    for copy in s_span:
        copy.wait()
    span_land(spad, 1)
    lax.fori_loop(1, cells - 1, second, 0)
    store_inner = pltpu.make_async_copy(
        qpad.at[:, pl.ds(2, cells - 2), inner], new_hbm.at[:, pl.ds(1, cells - 2)], out_sem.at[0]
    )
    store_inner.start()
    for copy in faces:
        copy.wait()
    lax.fori_loop(0, 2, lambda e, carry: second(e * (cells - 1), carry), 0)
    ends = []
    for e, i in enumerate((0, cells - 1)):
        copy = pltpu.make_async_copy(qpad.at[:, i + 1, inner], new_hbm.at[:, i], out_sem.at[1 + e])
        copy.start()
        ends.append(copy)
    store_inner.wait()
    for copy in ends:
        copy.wait()


def body(n_p, n_s, snapshots, snap_index, flow_state, eddy_viscosity, intersection, counts):
    start = flow_state[0]
    comps, cells, span, axial = start.shape
    halves = axial // LANES
    us = -(-6 * halves // n_p)
    units = us * n_p
    blocks = span // BLOCK
    tiles = span // ROWS_BF16
    f32 = jnp.float32
    pad = (comps, cells + 2, span + 16, axial)
    smem = pl.BlockSpec(memory_space=pltpu.SMEM)
    vmem = pl.BlockSpec(memory_space=pltpu.VMEM)
    hbm = pl.BlockSpec(memory_space=pltpu.HBM)
    dma = pltpu.SemaphoreType.DMA
    received, new = pl.pallas_call(
        functools.partial(couple_kernel, n_p, n_s, 1.0 / (SNAPS * cells * n_p)),
        out_shape=(
            jax.ShapeDtypeStruct((6, span, axial), f32),
            jax.ShapeDtypeStruct(start.shape, f32),
        ),
        in_specs=[smem, smem, smem, hbm, hbm, hbm],
        out_specs=(vmem, pl.BlockSpec(memory_space=pl.ANY)),
        scratch_shapes=[
            pltpu.VMEM((snapshots.shape[1], 3, cells, ROWS_BF16, axial), snapshots.dtype),
            pltpu.VMEM((snapshots.shape[1], 3, cells, ROWS_BF16, axial), snapshots.dtype),
            pltpu.VMEM((units, span, LANES), f32),
            pltpu.VMEM((n_p, us, span, LANES), f32),
            pltpu.VMEM((us, blocks, BLOCK, LANES), f32),
            pltpu.VMEM((n_s, CAPACITY, us, BLOCK, LANES), f32),
            pltpu.VMEM((n_s, CAPACITY, us, BLOCK, LANES), f32),
            pltpu.VMEM((units, span, LANES), f32),
            pltpu.VMEM(pad, f32),
            pltpu.VMEM(pad, f32),
            pltpu.VMEM((3, cells, span, axial), f32),
            pltpu.VMEM((cells, span, axial), f32),
            pltpu.VMEM((span, axial), f32),
            pltpu.VMEM((3, span, axial), f32),
            pltpu.VMEM((2, 2, comps, cells, axial), f32),
            pltpu.VMEM((2, 2, comps, cells, axial), f32),
            dma((n_p, tiles)), dma((n_p, tiles)),
            dma((n_s,)), dma((n_s,)), dma((n_p,)), dma((n_p,)),
            dma((4,)), dma((4,)), dma((2, 2)), dma((2, 2)), dma((2,)), dma((tiles,)), dma((3,)),
        ],
        compiler_params=pltpu.CompilerParams(
            collective_id=0, has_side_effects=True, vmem_limit_bytes=40 * 1024 * 1024
        ),
    )(snap_index, intersection[0], counts[0], snapshots[0], start, eddy_viscosity[0])
    return (received[None], new[None])


def solution(mesh):
    return jax.shard_map(
        functools.partial(body, mesh.shape["pitch"], mesh.shape["span"]),
        mesh=mesh,
        in_specs=(
            P("row", None, None, "pitch", "span", None),
            P(),
            P("row", None, "pitch", "span", None),
            P("row", "pitch", "span", None),
            P("row", None),
            P("row", None),
        ),
        out_specs=(P("row", None, "span", None), P("row", None, "pitch", "span", None)),
        check_vma=False,
    )
```

```python
import functools

import jax
import jax.numpy as jnp
from jax import lax
from jax.experimental import pallas as pl
from jax.experimental.pallas import tpu as pltpu
from jax.sharding import PartitionSpec as P

SNAPS = 16
BLOCK = 8
CAPACITY = 2
LANES = 128
ROWS_BF16 = 16
MESH = pl.DeviceIdType.MESH

stress_pairs = ((0, 0), (0, 1), (0, 2), (1, 1), (1, 2), (2, 2))
time_step = 0.1


def stress_tile(snaps, slots, mean, part, rows):
    cells = mean.shape[1]
    halves = mean.shape[3] // LANES
    for h in range(halves):
        cols = slice(h * LANES, (h + 1) * LANES)

        def one(i, acc):
            def load(t):
                return [snaps[slots[t], c, i, :, cols].astype(jnp.float32) for c in range(3)]

            base = load(0)
            sums, prods = None, None
            for t in range(1, SNAPS):
                now = load(t)
                d = [now[c] - base[c] for c in range(3)]
                pr = [d[p] * d[q] for p, q in stress_pairs]
                sums = d if sums is None else [a + b for a, b in zip(sums, d)]
                prods = pr if prods is None else [a + b for a, b in zip(prods, pr)]
            shift = [s * (1.0 / SNAPS) for s in sums]
            for c in range(3):
                mean[c, i, rows, cols] = base[c] + shift[c]
            return tuple(
                a + (pr - sums[p] * shift[q]) for a, pr, (p, q) in zip(acc, prods, stress_pairs)
            )

        zero = jnp.zeros((ROWS_BF16, LANES), jnp.float32)
        acc = lax.fori_loop(0, cells, one, (zero,) * 6)
        for m in range(6):
            part[m * halves + h, rows] = acc[m]
    for u in range(6 * halves, part.shape[0]):
        part[u, rows] = jnp.zeros((ROWS_BF16, LANES), jnp.float32)


def next_cell(x):
    lane = lax.broadcasted_iota(jnp.int32, x.shape, 1)
    return jnp.where(lane == x.shape[1] - 1, x, pltpu.roll(x, x.shape[1] - 1, 1))


def last_cell(x):
    lane = lax.broadcasted_iota(jnp.int32, x.shape, 1)
    return jnp.where(lane == 0, x, pltpu.roll(x, 1, 1))


def couple_kernel(
    n_p, n_s, scale,
    slot_list, links, counts, snaps_hbm, q_hbm, visc_hbm,
    rec_out, new_hbm,
    snaps_even, snaps_odd, part, rs_buf, tot, out_buf, a2a, rec, qpad, spad, mean, visc, dtm, src,
    zsend, zrecv,
    rs_s, rs_r, aa_s, aa_r, ag_s, ag_r, hp_s, hp_r, hz_s, hz_r, loc, snap_sem, out_sem,
):
    r, p, s = lax.axis_index("row"), lax.axis_index("pitch"), lax.axis_index("span")
    comps, cells, span, axial = q_hbm.shape
    us = part.shape[0] // n_p
    blocks = span // BLOCK
    halves = axial // LANES
    tile = ROWS_BF16
    top = 8

    tiles = span // tile

    snaps = (snaps_even, snaps_odd)

    def load_snaps(j):
        return pltpu.make_async_copy(
            snaps_hbm.at[:, :, :, pl.ds(j * tile, tile)], snaps[j % 2], snap_sem.at[j]
        )

    loads = [load_snaps(j) for j in range(tiles)]
    loads[0].start()
    load_q = pltpu.make_async_copy(
        q_hbm, qpad.at[:, pl.ds(1, cells), pl.ds(top, span)], loc.at[0]
    )
    load_q.start()
    load_visc = pltpu.make_async_copy(visc_hbm, visc, loc.at[1])
    load_visc.start()
    loads[1].start()

    barrier = pltpu.get_barrier_semaphore()
    for d in range(n_p):
        to = lax.rem(p + d, n_p)
        pl.semaphore_signal(barrier, inc=1, device_id=(1 - r, to, s), device_id_type=MESH)
        if d:
            pl.semaphore_signal(barrier, inc=1, device_id=(r, to, s), device_id_type=MESH)
    for d in range(1, n_s):
        to = lax.rem(s + d, n_s)
        pl.semaphore_signal(barrier, inc=1, device_id=(r, p, to), device_id_type=MESH)
    pl.semaphore_wait(barrier, 2 * n_p + n_s - 2)

    right, left = lax.rem(p + 1, n_p), lax.rem(p + n_p - 1, n_p)
    above, below = lax.rem(s + 1, n_s), lax.rem(s + n_s - 1, n_s)
    high_q = pltpu.make_async_remote_copy(
        src_ref=q_hbm.at[:, 0], dst_ref=qpad.at[:, cells + 1, pl.ds(top, span)],
        send_sem=hp_s.at[0], recv_sem=hp_r.at[0],
        device_id=(r, left, s), device_id_type=MESH,
    )
    low_q = pltpu.make_async_remote_copy(
        src_ref=q_hbm.at[:, cells - 1], dst_ref=qpad.at[:, 0, pl.ds(top, span)],
        send_sem=hp_s.at[3], recv_sem=hp_r.at[3],
        device_id=(r, right, s), device_id_type=MESH,
    )
    low_q.start()

    def span_faces(pad, k):
        def pack(i, carry):
            for c in range(comps):
                zsend[k, 0, c, pl.ds(i, 1)] = pad[c, i + 1, top + span - 1 : top + span]
                zsend[k, 1, c, pl.ds(i, 1)] = pad[c, i + 1, top : top + 1]
            return carry

        lax.fori_loop(0, cells, pack, 0)
        copies = []
        for way, to in ((0, above), (1, below)):
            copies.append(pltpu.make_async_remote_copy(
                src_ref=zsend.at[k, way], dst_ref=zrecv.at[k, way],
                send_sem=hz_s.at[k, way], recv_sem=hz_r.at[k, way],
                device_id=(r, p, to), device_id_type=MESH,
            ))
        for copy in copies:
            copy.start()
        return copies

    def span_land(pad, k):
        def land(i, carry):
            for c in range(comps):
                row = zrecv[k, 0, c, pl.ds(i, 1)]
                pad[c, i + 1, top - 1 : top] = jnp.where(s == 0, jnp.zeros_like(row), row)
                row = zrecv[k, 1, c, pl.ds(i, 1)]
                pad[c, i + 1, top + span : top + span + 1] = jnp.where(
                    s == n_s - 1, jnp.zeros_like(row), row
                )
            return carry

        lax.fori_loop(0, cells, land, 0)

    load_q.wait()
    q_span = span_faces(qpad, 0)

    slots = [slot_list[t] for t in range(SNAPS)]
    scatter = []
    for j in range(tiles):
        loads[j].wait()
        stress_tile(snaps[j % 2], slots, mean, part, slice(j * tile, (j + 1) * tile))
        if j + 2 < tiles:
            loads[j + 2].start()
        for d in range(n_p):
            to = lax.rem(p + d, n_p)
            copy = pltpu.make_async_remote_copy(
                src_ref=part.at[pl.ds(to * us, us), pl.ds(j * tile, tile)],
                dst_ref=rs_buf.at[d, :, pl.ds(j * tile, tile)],
                send_sem=rs_s.at[d, j], recv_sem=rs_r.at[d, j],
                device_id=(1 - r, to, s), device_id_type=MESH,
            )
            copy.start()
            scatter.append(copy)
    high_q.start()

    for j in range(span // tile):
        row = lax.broadcasted_iota(jnp.int32, (tile, axial), 0)
        first = counts[s * blocks + 2 * j]
        second = counts[s * blocks + 2 * j + 1]
        limit = jnp.where(row < BLOCK, first, second + BLOCK)
        dtm[j * tile : (j + 1) * tile] = jnp.where(row < limit, time_step, 0.0).astype(jnp.float32)

    for copy in scatter:
        copy.wait()
    for b in range(blocks):
        for u in range(us):
            total = rs_buf[0, u, b * BLOCK : (b + 1) * BLOCK]
            for d in range(1, n_p):
                total = total + rs_buf[d, u, b * BLOCK : (b + 1) * BLOCK]
            tot[u, b] = total * scale

    exchange = []
    for d in range(n_s):
        to = lax.rem(s + d, n_s)
        count = jnp.int32(0)
        picks = [jnp.int32(0)] * CAPACITY
        for k in range(blocks):
            block = links[to * blocks + k]
            here = block // blocks == s
            inside = block % blocks
            for c in range(CAPACITY):
                picks[c] = jnp.where(here & (count == c), inside, picks[c])
            count = count + here.astype(jnp.int32)
        for c in range(CAPACITY):
            for u in range(us):
                if d == 0:
                    a2a[0, c, u] = tot[u, picks[c]]
                else:
                    out_buf[d, c, u] = tot[u, picks[c]]
        if d:
            copy = pltpu.make_async_remote_copy(
                src_ref=out_buf.at[d], dst_ref=a2a.at[d],
                send_sem=aa_s.at[d], recv_sem=aa_r.at[d],
                device_id=(r, p, to), device_id_type=MESH,
            )
            copy.start()
            exchange.append(copy)
    sources = [links[s * blocks + k] // blocks for k in range(blocks)]
    for copy in exchange:
        copy.wait()
    for k in range(blocks):
        slot = jnp.int32(0)
        for e in range(k):
            slot = slot + (sources[e] == sources[k]).astype(jnp.int32)
        slot = jnp.minimum(slot, CAPACITY - 1)
        away = lax.rem(s - sources[k] + n_s, n_s)
        for u in range(us):
            rec[p * us + u, k * BLOCK : (k + 1) * BLOCK] = a2a[away, slot, u]
    gather = []
    for d in range(1, n_p):
        to = lax.rem(p + d, n_p)
        copy = pltpu.make_async_remote_copy(
            src_ref=rec.at[pl.ds(p * us, us)], dst_ref=rec.at[pl.ds(p * us, us)],
            send_sem=ag_s.at[d], recv_sem=ag_r.at[d],
            device_id=(r, to, s), device_id_type=MESH,
        )
        copy.start()
        gather.append(copy)

    for copy in q_span:
        copy.wait()
    span_land(qpad, 0)
    load_visc.wait()
    low_q.wait()
    high_q.wait()
    for copy in gather:
        copy.wait()

    for j in range(span // tile):
        rows = slice(j * tile, (j + 1) * tile)
        t = [
            jnp.concatenate([rec[m * halves + h, rows] for h in range(halves)], axis=1)
            for m in range(6)
        ]
        for m in range(6):
            rec_out[m, rows] = t[m]
        row = lax.broadcasted_iota(jnp.int32, (tile, axial), 0) + (s * span + j * tile)
        curve = 1.0 / (1.0 + (row.astype(jnp.float32) + 0.5) / (span * n_s))
        diff = [(next_cell(t[m]) - last_cell(t[m])) * 0.5 for m in range(3)]
        live = dtm[rows]
        src[0, rows] = live * (-diff[0] - curve * t[1])
        src[1, rows] = live * (-diff[1] + curve * (t[5] - t[3]))
        src[2, rows] = live * (-diff[2] - 2.0 * curve * t[4])

    def section(pad, i, finish):
        for j in range(span // BLOCK):
            rows = slice(j * BLOCK, (j + 1) * BLOCK)
            nu = visc[i, rows]
            means = [mean[c, i, rows] for c in range(3)]
            speed = 0.5 + means[0]
            live = dtm[rows]
            ahead = live * (nu - 0.5 * next_cell(speed))
            behind = live * (nu + 0.5 * last_cell(speed))
            nu = live * nu
            force = [src[c, rows] for c in range(3)]
            energy = means[0] * force[0] + means[1] * force[1] + means[2] * force[2]
            force = [None] + force + [energy]
            steps = []
            at = top + j * BLOCK
            for c in range(comps):
                x = pad[c, i + 1, at : at + BLOCK]
                around = (
                    pad[c, i, at : at + BLOCK] + pad[c, i + 2, at : at + BLOCK]
                    + pad[c, i + 1, at - 1 : at + BLOCK - 1]
                    + pad[c, i + 1, at + 1 : at + BLOCK + 1]
                )
                step = (
                    ahead * next_cell(x) + behind * last_cell(x) + nu * (around - 6.0 * x)
                )
                if force[c] is not None:
                    step = step + force[c]
                steps.append((x, step))
            finish(i, at, steps)

    def first(i, carry):
        def finish(i, at, steps):
            for c, (x, step) in enumerate(steps):
                spad[c, i + 1, at : at + BLOCK] = x + step

        section(qpad, i, finish)
        return carry

    outs = []

    def second(i, carry):
        def finish(i, at, steps):
            ends = [
                0.5 * (qpad[c, i + 1, at : at + BLOCK] + x + step)
                for c, (x, step) in enumerate(steps)
            ]
            for c, end in enumerate(ends):
                qpad[c, i + 1, at : at + BLOCK] = end

        section(spad, i, finish)
        return carry

    inner = pl.ds(top, span)
    lax.fori_loop(0, 2, lambda e, carry: first(e * (cells - 1), carry), 0)
    faces = []
    for way, (mine, theirs, to) in enumerate(((cells, 0, right), (1, cells + 1, left))):
        copy = pltpu.make_async_remote_copy(
            src_ref=spad.at[:, mine, inner], dst_ref=spad.at[:, theirs, inner],
            send_sem=hp_s.at[1 + way], recv_sem=hp_r.at[1 + way],
            device_id=(r, to, s), device_id_type=MESH,
        )
        copy.start()
        faces.append(copy)
    lax.fori_loop(1, cells - 1, first, 0)
    s_span = span_faces(spad, 1)
    for copy in s_span:
        copy.wait()
    span_land(spad, 1)
    lax.fori_loop(1, cells - 1, second, 0)
    store_inner = pltpu.make_async_copy(
        qpad.at[:, pl.ds(2, cells - 2), inner], new_hbm.at[:, pl.ds(1, cells - 2)], out_sem.at[0]
    )
    store_inner.start()
    for copy in faces:
        copy.wait()
    lax.fori_loop(0, 2, lambda e, carry: second(e * (cells - 1), carry), 0)
    ends = []
    for e, i in enumerate((0, cells - 1)):
        copy = pltpu.make_async_copy(qpad.at[:, i + 1, inner], new_hbm.at[:, i], out_sem.at[1 + e])
        copy.start()
        ends.append(copy)
    store_inner.wait()
    for copy in ends:
        copy.wait()


def body(n_p, n_s, snapshots, snap_index, flow_state, eddy_viscosity, intersection, counts):
    start = flow_state[0]
    comps, cells, span, axial = start.shape
    halves = axial // LANES
    us = -(-6 * halves // n_p)
    units = us * n_p
    blocks = span // BLOCK
    tiles = span // ROWS_BF16
    f32 = jnp.float32
    pad = (comps, cells + 2, span + 16, axial)
    smem = pl.BlockSpec(memory_space=pltpu.SMEM)
    vmem = pl.BlockSpec(memory_space=pltpu.VMEM)
    hbm = pl.BlockSpec(memory_space=pltpu.HBM)
    dma = pltpu.SemaphoreType.DMA
    received, new = pl.pallas_call(
        functools.partial(couple_kernel, n_p, n_s, 1.0 / (SNAPS * cells * n_p)),
        out_shape=(
            jax.ShapeDtypeStruct((6, span, axial), f32),
            jax.ShapeDtypeStruct(start.shape, f32),
        ),
        in_specs=[smem, smem, smem, hbm, hbm, hbm],
        out_specs=(vmem, pl.BlockSpec(memory_space=pl.ANY)),
        scratch_shapes=[
            pltpu.VMEM((snapshots.shape[1], 3, cells, ROWS_BF16, axial), snapshots.dtype),
            pltpu.VMEM((snapshots.shape[1], 3, cells, ROWS_BF16, axial), snapshots.dtype),
            pltpu.VMEM((units, span, LANES), f32),
            pltpu.VMEM((n_p, us, span, LANES), f32),
            pltpu.VMEM((us, blocks, BLOCK, LANES), f32),
            pltpu.VMEM((n_s, CAPACITY, us, BLOCK, LANES), f32),
            pltpu.VMEM((n_s, CAPACITY, us, BLOCK, LANES), f32),
            pltpu.VMEM((units, span, LANES), f32),
            pltpu.VMEM(pad, f32),
            pltpu.VMEM(pad, f32),
            pltpu.VMEM((3, cells, span, axial), f32),
            pltpu.VMEM((cells, span, axial), f32),
            pltpu.VMEM((span, axial), f32),
            pltpu.VMEM((3, span, axial), f32),
            pltpu.VMEM((2, 2, comps, cells, axial), f32),
            pltpu.VMEM((2, 2, comps, cells, axial), f32),
            dma((n_p, tiles)), dma((n_p, tiles)),
            dma((n_s,)), dma((n_s,)), dma((n_p,)), dma((n_p,)),
            dma((4,)), dma((4,)), dma((2, 2)), dma((2, 2)), dma((2,)), dma((tiles,)), dma((3,)),
        ],
        compiler_params=pltpu.CompilerParams(
            collective_id=0, has_side_effects=True, vmem_limit_bytes=40 * 1024 * 1024
        ),
    )(snap_index, intersection[0], counts[0], snapshots[0], start, eddy_viscosity[0])
    return (received[None], new[None])


def solution(mesh):
    return jax.shard_map(
        functools.partial(body, mesh.shape["pitch"], mesh.shape["span"]),
        mesh=mesh,
        in_specs=(
            P("row", None, None, "pitch", "span", None),
            P(),
            P("row", None, "pitch", "span", None),
            P("row", "pitch", "span", None),
            P("row", None),
            P("row", None),
        ),
        out_specs=(P("row", None, "span", None), P("row", None, "pitch", "span", None)),
        check_vma=False,
    )
```
